32 devices in a mesh: groups: 2 (over y), cell: 4 (over z), member: 4 (over x, core).
Axes of the slice: x: 2, y: 2, z: 4, core: 2. Of those that a mesh axis runs over, the one named last changes fastest.
Arguments:
- prior_sample_set: float32 [512, 3, 32, 512], P(('groups', 'member'), None, 'cell'), parts along dimension 0, may hold values from -6 to 6
- wind_table: float32 [8, 2], replicated, may hold values from -0.45 to 0.45
- regimes: int32 [16, 4], P('groups'), parts along dimension 0, may hold values from 0 to 7
- obs_index: int32 [8, 512], P(('groups', 'cell')), parts along dimension 0, may hold values from 0 to 4095
- obs_count: int32 [8], P(('groups', 'cell')), parts along dimension 0, may hold values from 1 to 512, as said below
- obs_value: float32 [8, 512], P(('groups', 'cell')), parts along dimension 0, may hold values from -6 to 6
- obs_var: float32 [8, 512], P(('groups', 'cell')), parts along dimension 0, may hold values from 0.25 to 4
Outputs:
- posterior_sample_set: float32 [512, 3, 32, 512], P(('groups', 'member'), None, 'cell'), parts along dimension 0
The draws below stay inside these ranges and needn't reach their ends.
There are 2 independent parts, one for each index of `groups`. The reference program is written for one: setup_inputs(seed, part) draws one part's arguments, and reference() takes and returns one part's arrays. A program takes and returns all parts, laid end to end along the dimension named above; an argument that names none is the same for every part. Nothing has to cross between parts.
Inputs may be any that keep to these rules, and one draw needn't show every extreme that they name: `obs_count`: some tile has exactly 512 live slots.
All inputs are finite; a program needn't handle non-finite values.
Results may differ from the reference program's by a relative error of at most 0.019.
The reference program's roundings to bfloat16 on the way count: a program that leaves them out, or rounds other values in their place, can miss the bound.
Values may be sent and summed in bfloat16 or wider, within the bound.
A program may use at most 64 MiB of HBM per device.

```python
import math
import jax
import jax.numpy as jnp
from jax import lax

REALIZATION_NUM = 256
FIELDS = 3
MESH_WIDTH = 512
PATCH_HEIGHT = 8
SUBSTEPS = 4
BAND = 4
REGIMES = 8
OBS_T = 512
ROOT_STEPS = 24
NX = 32
N_CELL = 4


def draw_obs_count(key, part):
    counts = jax.random.randint(jax.random.fold_in(key, 11), (N_CELL,), 1, OBS_T + 1)
    full_tile = jax.random.randint(jax.random.fold_in(key, 12), (), 0, N_CELL)
    return jnp.where(jnp.arange(N_CELL) == full_tile, OBS_T, counts).astype(jnp.int32)


def draw_prior_sample_set(key, part):
    shape_full = (REALIZATION_NUM, FIELDS, NX, MESH_WIDTH)
    noise = jax.random.normal(jax.random.fold_in(key, 21), shape_full, jnp.float32)
    offset = 2.0 * jax.random.normal(jax.random.fold_in(key, 22), (REALIZATION_NUM, 1, 1, 1), jnp.float32)
    return jnp.clip(noise + offset, -6.0, 6.0).astype(jnp.float32)


def touch_ends(array, stream_key, smallest, high):
    shape = array.shape
    spot = [jax.random.randint(jax.random.fold_in(stream_key, axis), (), 0, shape[axis]) for axis in range(len(shape))]
    array = array.at[tuple(spot)].set(smallest)
    longest = shape.index(max(shape))
    spot[longest] = (spot[longest] + 1) % shape[longest]
    return array.at[tuple(spot)].set(high)


def steps_of(stream_key, shape, split, low, largest):
    def one(axis_at, blocks):
        steps = jax.random.uniform(jax.random.fold_in(jax.random.fold_in(stream_key, 6), axis_at), (blocks,), jnp.float32, low / len(split), largest / len(split))
        return jnp.repeat(jnp.exp(steps), shape[axis_at] // blocks).reshape((-1,) + (1,) * (len(shape) - axis_at - 1))

    loudness = one(*split[0])
    for cut in split[1:]:
        loudness = loudness * one(*cut)
    return loudness


def gaussian(key, extent, scale, reach, shards=(), kind=jnp.bfloat16):
    values = jax.random.normal(key, extent, jnp.float32) * scale
    if len(shards) > 0:
        values = steps_of(key, extent, shards, -0.22, 0.18) * values
    return jnp.clip(values, min=-reach, max=reach).astype(kind)


def setup_inputs(seed: int = 0, part: int = 0) -> dict:
    seeds = jax.random.split(jax.random.key(seed), 8)
    own_keys = jax.random.split(jax.random.fold_in(seeds[7], part), 8)
    prior_sample_set = draw_prior_sample_set(jax.random.fold_in(jax.random.fold_in(seeds[7], part), 71), part)
    wind_table = jnp.clip(jax.random.uniform(seeds[1], (REGIMES, 2), jnp.float32, -0.45, 0.45), -0.45, 0.45)
    regimes = touch_ends(jax.random.randint(own_keys[2], (NX // BAND, SUBSTEPS), 0, REGIMES), jax.random.fold_in(own_keys[2], 1), 0, REGIMES - 1).astype(jnp.int32)
    obs_index = touch_ends(jax.random.randint(own_keys[3], (N_CELL, OBS_T), 0, PATCH_HEIGHT * MESH_WIDTH), jax.random.fold_in(own_keys[3], 1), 0, (PATCH_HEIGHT * MESH_WIDTH) - 1).astype(jnp.int32)
    obs_count = draw_obs_count(jax.random.fold_in(jax.random.fold_in(seeds[7], part), 71), part)
    obs_value = gaussian(own_keys[5], (N_CELL, OBS_T), 1.0, 6.0, ((0, 4),), jnp.float32)
    obs_var = jnp.clip(jnp.exp(math.log(4.0) - 2.7725887 * jax.random.uniform(own_keys[6], (N_CELL, OBS_T), jnp.float32) ** steps_of(own_keys[6], (N_CELL, OBS_T), ((0, 4),), -0.2, 0.2)), 0.25, 4.0)
    return dict(prior_sample_set=prior_sample_set, wind_table=wind_table, regimes=regimes, obs_index=obs_index, obs_count=obs_count, obs_value=obs_value, obs_var=obs_var)


diffusion = 0.02

def row_speeds(row_ids, regime_column, wind_table, row_total):
    band_ids = jnp.clip(row_ids, 0, row_total - 1) // BAND
    band_hits = (band_ids[:, None] == jnp.arange(regime_column.shape[0])[None, :]).astype(jnp.int32)
    regime_ids = lax.optimization_barrier(jnp.sum(band_hits * regime_column[None, :], axis=1))
    regime_hits = (regime_ids[:, None] == jnp.arange(wind_table.shape[0])[None, :]).astype(jnp.float32)
    speed = jnp.dot(regime_hits, wind_table, precision=lax.Precision.HIGHEST, preferred_element_type=jnp.float32)
    return (speed[:, 0:1], speed[:, 1:2])

def stencil(padded, speed_x, speed_y):
    centre = padded[..., 1:-1, :]
    south = padded[..., :-2, :]
    north = padded[..., 2:, :]
    widths = [(0, 0)] * (centre.ndim - 1) + [(1, 1)]
    sides = jnp.pad(centre, widths)
    west = sides[..., :-2]
    east = sides[..., 2:]
    result = centre - jnp.maximum(speed_x, 0.0) * (centre - south) - jnp.minimum(speed_x, 0.0) * (north - centre)
    result = result - jnp.maximum(speed_y, 0.0) * (centre - west) - jnp.minimum(speed_y, 0.0) * (east - centre)
    return result + diffusion * (north + south + east + west - 4.0 * centre)

def inverse_root(precision_matrix):
    size_n = precision_matrix.shape[0]
    identity = jnp.eye(size_n, dtype=jnp.float32)
    scale = jnp.trace(precision_matrix)
    start = (precision_matrix / scale, identity)

    def newton_step(index, carry):
        upper, lower = carry
        middle = 1.5 * identity - 0.5 * jnp.dot(lower, upper, precision=lax.Precision.HIGHEST, preferred_element_type=jnp.float32)
        upper = jnp.dot(upper, middle, precision=lax.Precision.HIGHEST, preferred_element_type=jnp.float32)
        lower = jnp.dot(middle, lower, precision=lax.Precision.HIGHEST, preferred_element_type=jnp.float32)
        return (upper, lower)
    upper, lower = lax.fori_loop(0, ROOT_STEPS, newton_step, start)
    return (lower, scale)

def analysis(gram, gain, members):
    identity = jnp.eye(members, dtype=jnp.float32)
    precision_matrix = gram + (members - 1.0) * identity
    root_inverse, scale = inverse_root(precision_matrix)
    half_way = jnp.dot(root_inverse, gain, precision=lax.Precision.HIGHEST, preferred_element_type=jnp.float32)
    mean_weights = jnp.dot(root_inverse, half_way, precision=lax.Precision.HIGHEST, preferred_element_type=jnp.float32) / scale
    root = jnp.sqrt((members - 1.0) / scale) * root_inverse
    blend = mean_weights[:, None] + root
    transform = blend - lax.optimization_barrier(jnp.mean(blend, axis=0, keepdims=True)) + 1.0 / members
    return transform.astype(jnp.bfloat16)

def reference(prior_sample_set, wind_table, regimes, obs_index, obs_count, obs_value, obs_var):
    row_ids = jnp.arange(NX)
    speeds = [row_speeds(row_ids, regimes[:, step], wind_table, NX) for step in range(SUBSTEPS)]

    def predict_one_realization(realization_values):
        sample_set_values = realization_values
        for step in range(SUBSTEPS):
            padded = jnp.pad(sample_set_values, ((0, 0), (1, 1), (0, 0)))
            sample_set_values = stencil(padded, speeds[step][0], speeds[step][1])
        return sample_set_values
    predicted_values = lax.map(predict_one_realization, prior_sample_set)
    predicted_reduced_precise = predicted_values.astype(jnp.bfloat16)
    first_cloud_cover = predicted_values[:, 0].reshape(REALIZATION_NUM, N_CELL, PATCH_HEIGHT * MESH_WIDTH)
    predicted = first_cloud_cover[:, jnp.arange(N_CELL)[:, None], obs_index].reshape(REALIZATION_NUM, N_CELL * OBS_T)
    ybar = lax.optimization_barrier(jnp.mean(predicted, axis=0))
    spread = predicted - ybar[None, :]
    live = (jnp.arange(OBS_T)[None, :] < obs_count[:, None]).astype(jnp.float32)
    weight = (live / jnp.sqrt(obs_var)).reshape(-1)
    scaled = spread * weight[None, :]
    gram = jnp.dot(scaled, scaled.T, precision=lax.Precision.HIGHEST, preferred_element_type=jnp.float32)
    innovation = weight * (obs_value.reshape(-1) - ybar)
    gain = jnp.dot(scaled, innovation, precision=lax.Precision.HIGHEST, preferred_element_type=jnp.float32)
    update_matrix_reduced_precise = analysis(gram, gain, REALIZATION_NUM)
    posterior_sample_set = jnp.dot(update_matrix_reduced_precise.T, predicted_reduced_precise.reshape(REALIZATION_NUM, -1), preferred_element_type=jnp.float32)
    return posterior_sample_set.reshape(REALIZATION_NUM, FIELDS, NX, MESH_WIDTH)
```

```python
import functools

import jax
import jax.numpy as jnp
from jax import lax
from jax.experimental import pallas as pl
from jax.experimental.pallas import tpu as pltpu
from jax.sharding import PartitionSpec as P

SUBSTEPS = 4
BAND = 4
ROOT_STEPS = 24
HALO = SUBSTEPS
DIFFUSION = 0.02
MESH = pl.DeviceIdType.MESH
HIGHEST = lax.Precision.HIGHEST
VMEM_LIMIT = 48 * 1024 * 1024


def stencil_coeffs(regimes, wind_table, first_row, tile_rows, row_total):
    row_ids = first_row - HALO + jnp.arange(tile_rows + 2 * HALO)
    band_ids = jnp.clip(row_ids, 0, row_total - 1) // BAND
    band_hits = band_ids[:, None, None] == jnp.arange(regimes.shape[0])[None, :, None]
    ids = jnp.sum(jnp.where(band_hits, regimes[None], 0), axis=1)
    hits = ids[:, :, None, None] == jnp.arange(wind_table.shape[0])[None, None, :, None]
    speed = jnp.sum(jnp.where(hits, wind_table[None, None], 0.0), axis=2)
    cx, cy = speed[:, :, 0], speed[:, :, 1]
    parts = [
        1.0 - jnp.abs(cx) - jnp.abs(cy) - 4.0 * DIFFUSION,
        jnp.maximum(cx, 0.0) + DIFFUSION,
        DIFFUSION - jnp.minimum(cx, 0.0),
        jnp.maximum(cy, 0.0) + DIFFUSION,
        DIFFUSION - jnp.minimum(cy, 0.0),
    ]
    inside = (row_ids >= 0) & (row_ids < row_total)
    table = jnp.where(inside[:, None, None], jnp.stack(parts, axis=2), 0.0)
    return table.reshape(row_ids.shape[0], SUBSTEPS * 5).T


def stencil_kernel(chunk, with_obs, coeff_ref, *refs):
    if with_obs:
        index_ref, x_ref, south_ref, north_ref, out_ref, pred_ref, keep = refs
    else:
        x_ref, south_ref, north_ref, out_ref = refs
    rows, members, width = x_ref.shape[1:]
    lane = lax.broadcasted_iota(jnp.int32, (chunk, width), 1)

    def one_chunk(step_at, carry):
        at = pl.ds(pl.multiple_of(step_at * chunk, chunk), chunk)
        cells = [south_ref[0, i, at, :].astype(jnp.float32) for i in range(HALO)]
        cells += [x_ref[0, i, at, :] for i in range(rows)]
        cells += [north_ref[0, i, at, :].astype(jnp.float32) for i in range(HALO)]
        for s in range(SUBSTEPS):
            fresh = list(cells)
            for i in range(s + 1, rows + 2 * HALO - s - 1):
                q = cells[i]
                west = jnp.where(lane == 0, 0.0, pltpu.roll(q, 1, 1))
                east = jnp.where(lane == width - 1, 0.0, pltpu.roll(q, width - 1, 1))
                fresh[i] = (
                    q * coeff_ref[s * 5, i]
                    + cells[i - 1] * coeff_ref[s * 5 + 1, i]
                    + cells[i + 1] * coeff_ref[s * 5 + 2, i]
                    + west * coeff_ref[s * 5 + 3, i]
                    + east * coeff_ref[s * 5 + 4, i]
                )
            cells = fresh
        for i in range(rows):
            out_ref[0, i, at, :] = cells[HALO + i].astype(jnp.bfloat16)
            if with_obs:
                keep[i, at, :] = cells[HALO + i]
        return carry

    lax.fori_loop(0, members // chunk, one_chunk, 0)
    if with_obs:
        slots = index_ref.shape[1]
        column = lax.broadcasted_iota(jnp.int32, (width, slots), 0)
        pred_ref[...] = jnp.zeros_like(pred_ref)

        def one_row(i, carry):
            hits = jnp.where(column == index_ref[...] - i * width, 1.0, 0.0).astype(jnp.bfloat16)
            value = keep[i]
            high = value.astype(jnp.bfloat16)
            rest = value - high.astype(jnp.float32)
            middle = rest.astype(jnp.bfloat16)
            low = (rest - middle.astype(jnp.float32)).astype(jnp.bfloat16)
            picked = jnp.dot(
                jnp.concatenate([high, middle, low], axis=0),
                hits,
                preferred_element_type=jnp.float32,
            )
            pred_ref[...] += (
                picked[:members] + picked[members : 2 * members] + picked[2 * members :]
            )
            return carry

        lax.fori_loop(0, rows, one_row, 0)


def stencil_call(coeffs, cells, south, north, obs_index=None):
    fields, rows, members, width = cells.shape
    with_obs = obs_index is not None
    chunk = 16
    block = lambda r: pl.BlockSpec((1, r, members, width), lambda f: (f, 0, 0, 0))
    in_specs = [pl.BlockSpec(memory_space=pltpu.SMEM)]
    args = [coeffs]
    out_shape = [jax.ShapeDtypeStruct(cells.shape, jnp.bfloat16)]
    out_specs = [block(rows)]
    scratch = []
    if with_obs:
        slots = obs_index.shape[1]
        in_specs.append(pl.BlockSpec((1, slots), lambda f: (0, 0)))
        args.append(obs_index)
        out_shape.append(jax.ShapeDtypeStruct((members, slots), jnp.float32))
        out_specs.append(pl.BlockSpec((members, slots), lambda f: (0, 0)))
        scratch.append(pltpu.VMEM((rows, members, width), jnp.float32))
    return pl.pallas_call(
        functools.partial(stencil_kernel, chunk, with_obs),
        grid=(fields,),
        in_specs=in_specs + [block(rows), block(HALO), block(HALO)],
        out_specs=out_specs,
        out_shape=out_shape,
        scratch_shapes=scratch,
        compiler_params=pltpu.CompilerParams(vmem_limit_bytes=VMEM_LIMIT),
        cost_estimate=pl.CostEstimate(
            flops=fields * 60 * members * width * 12,
            bytes_accessed=fields * members * width * rows * 8,
            transcendentals=0,
        ),
    )(*args, cells, south, north)


def nt_dot(a, b):
    return lax.dot_general(
        a, b, (((1,), (1,)), ((), ())), precision=HIGHEST, preferred_element_type=jnp.float32
    )


def nn_dot(a, b):
    return jnp.dot(a, b, precision=HIGHEST, preferred_element_type=jnp.float32)


def analysis_kernel(
    n_cell,
    n_member,
    pred_ref,
    weight_ref,
    value_ref,
    out_ref,
    everyone,
    mine,
    others,
    total,
    gram,
    upper,
    lower,
    send_pred,
    recv_pred,
    send_part,
    recv_part,
    send_gram,
    recv_gram,
):
    cell = lax.axis_index("cell")
    member = lax.axis_index("member")
    count = pred_ref.shape[0]
    members = count * n_member

    barrier = pltpu.get_barrier_semaphore()
    for d in range(1, n_member):
        pl.semaphore_signal(
            barrier, inc=1, device_id={"member": lax.rem(member + d, n_member)}, device_id_type=MESH
        )
    for d in range(1, n_cell):
        pl.semaphore_signal(
            barrier, inc=1, device_id={"cell": lax.rem(cell + d, n_cell)}, device_id_type=MESH
        )
    pl.semaphore_wait(barrier, n_member + n_cell - 2)

    own = pl.ds(pl.multiple_of(member * count, count), count)
    copies = []
    for d in range(1, n_member):
        copy = pltpu.make_async_remote_copy(
            src_ref=pred_ref,
            dst_ref=everyone.at[own],
            send_sem=send_pred.at[d],
            recv_sem=recv_pred.at[d],
            device_id={"member": lax.rem(member + d, n_member)},
            device_id_type=MESH,
        )
        copy.start()
        copies.append(copy)
    everyone[own, :] = pred_ref[...]
    for copy in copies:
        copy.wait()

    predicted = everyone[...]
    ybar = jnp.mean(predicted, axis=0, keepdims=True)
    weight = weight_ref[...]
    scaled = (predicted - ybar) * weight
    local = (pred_ref[...] - ybar) * weight
    innovation = jnp.broadcast_to(weight * (value_ref[...] - ybar), (8, weight.shape[1]))
    mine[...] = nt_dot(jnp.concatenate([local, innovation], axis=0), scaled)

    copies = []
    for d in range(1, n_cell):
        copy = pltpu.make_async_remote_copy(
            src_ref=mine,
            dst_ref=others.at[d - 1],
            send_sem=send_part.at[d],
            recv_sem=recv_part.at[d],
            device_id={"cell": lax.rem(cell + d, n_cell)},
            device_id_type=MESH,
        )
        copy.start()
        copies.append(copy)
    for copy in copies:
        copy.wait()
    summed = mine[...]
    for d in range(n_cell - 1):
        summed = summed + others[d]
    total[...] = summed

    copies = []
    for d in range(1, n_member):
        copy = pltpu.make_async_remote_copy(
            src_ref=total.at[pl.ds(0, count)],
            dst_ref=gram.at[own],
            send_sem=send_gram.at[d],
            recv_sem=recv_gram.at[d],
            device_id={"member": lax.rem(member + d, n_member)},
            device_id_type=MESH,
        )
        copy.start()
        copies.append(copy)
    gram[own, :] = total[pl.ds(0, count), :]
    for copy in copies:
        copy.wait()

    rows = lax.broadcasted_iota(jnp.int32, (members, members), 0)
    columns = lax.broadcasted_iota(jnp.int32, (members, members), 1)
    identity = jnp.where(rows == columns, 1.0, 0.0).astype(jnp.float32)
    precision = gram[...] + (members - 1.0) * identity
    scale = jnp.sum(jnp.sum(precision * identity, axis=1, keepdims=True), axis=0, keepdims=True)
    upper[...] = precision / scale
    lower[...] = identity

    def newton(step, carry):
        middle = 1.5 * identity - 0.5 * nn_dot(lower[...], upper[...])
        upper[...] = nn_dot(upper[...], middle)
        lower[...] = nn_dot(middle, lower[...])
        return carry

    lax.fori_loop(0, ROOT_STEPS, newton, 0)

    gain = total[pl.ds(count, 8), :]
    half_way = nt_dot(gain, lower[...])
    mean_weights = nt_dot(half_way, lower[...])[0:1, :] / scale
    root = jnp.sqrt((members - 1.0) / scale) * lower[own, :]
    blend = mean_weights + root
    transform = blend - jnp.mean(blend, axis=1, keepdims=True) + 1.0 / members
    out_ref[...] = transform.astype(jnp.bfloat16)


def analysis_call(local_pred, weight, value):
    n_cell, n_member = lax.axis_size("cell"), lax.axis_size("member")
    count, slots = local_pred.shape
    members = count * n_member
    vmem = pl.BlockSpec(memory_space=pltpu.VMEM)
    dma = pltpu.SemaphoreType.DMA
    return pl.pallas_call(
        functools.partial(analysis_kernel, n_cell, n_member),
        out_shape=jax.ShapeDtypeStruct((count, members), jnp.bfloat16),
        in_specs=[vmem] * 3,
        out_specs=vmem,
        scratch_shapes=[
            pltpu.VMEM((members, slots), jnp.float32),
            pltpu.VMEM((count + 8, members), jnp.float32),
            pltpu.VMEM((n_cell - 1, count + 8, members), jnp.float32),
            pltpu.VMEM((count + 8, members), jnp.float32),
            pltpu.VMEM((members, members), jnp.float32),
            pltpu.VMEM((members, members), jnp.float32),
            pltpu.VMEM((members, members), jnp.float32),
            dma((n_member,)),
            dma((n_member,)),
            dma((n_cell,)),
            dma((n_cell,)),
            dma((n_member,)),
            dma((n_member,)),
        ],
        compiler_params=pltpu.CompilerParams(
            collective_id=0, has_side_effects=True, vmem_limit_bytes=16 * 1024 * 1024
        ),
        cost_estimate=pl.CostEstimate(
            flops=ROOT_STEPS * 3 * 12 * members**3, bytes_accessed=1 << 20, transcendentals=0
        ),
    )(local_pred, weight, value)


def blend_kernel(coeff_ref, piece_ref, out_ref):
    n_member, _, rows, count, width = piece_ref.shape
    for r in range(rows):
        block = piece_ref[:, 0, r].reshape(n_member * count, width)
        out_ref[0, r] = jnp.dot(coeff_ref[...], block, preferred_element_type=jnp.float32)


def blend_call(transform, piece):
    n_member, fields, rows, count, width = piece.shape
    group = rows // 2 if rows % 2 == 0 else rows
    return pl.pallas_call(
        blend_kernel,
        grid=(fields, rows // group),
        in_specs=[
            pl.BlockSpec(transform.shape, lambda f, r: (0, 0)),
            pl.BlockSpec((n_member, 1, group, count, width), lambda f, r: (0, f, r, 0, 0)),
        ],
        out_specs=pl.BlockSpec((1, group, count, width), lambda f, r: (f, r, 0, 0)),
        out_shape=jax.ShapeDtypeStruct((fields, rows, count, width), jnp.float32),
        compiler_params=pltpu.CompilerParams(vmem_limit_bytes=VMEM_LIMIT),
    )(transform, piece)


def halos(cells):
    n_cell = lax.axis_size("cell")
    rows = cells.shape[1]
    up = [(i, i + 1) for i in range(n_cell - 1)]
    down = [(i + 1, i) for i in range(n_cell - 1)]
    south = lax.ppermute(cells[:, rows - HALO :].astype(jnp.bfloat16), "cell", up)
    north = lax.ppermute(cells[:, :HALO].astype(jnp.bfloat16), "cell", down)
    return south, north


def shards(prior_sample_set, wind_table, regimes, obs_index, obs_count, obs_value, obs_var):
    tile_rows = prior_sample_set.shape[2]
    row_total = tile_rows * lax.axis_size("cell")
    first_row = lax.axis_index("cell") * tile_rows
    coeffs = stencil_coeffs(regimes, wind_table, first_row, tile_rows, row_total)
    live = jnp.arange(obs_var.shape[1])[None, :] < obs_count[0]
    weight = live.astype(jnp.float32) / jnp.sqrt(obs_var)

    cells = prior_sample_set.transpose(1, 2, 0, 3)
    south, north = halos(cells[:1])
    south_rest, north_rest = halos(cells[1:])
    first, local_pred = stencil_call(coeffs, cells[:1], south, north, obs_index)
    (rest,) = stencil_call(coeffs, cells[1:], south_rest, north_rest)
    transform = analysis_call(local_pred, weight, obs_value)
    piece = lax.all_gather(jnp.concatenate([first, rest], axis=0), "member", axis=0, tiled=False)
    blended = blend_call(transform, piece)
    return blended.transpose(2, 0, 1, 3)


def solution(mesh):
    return jax.shard_map(
        shards,
        mesh=mesh,
        in_specs=(
            P(("groups", "member"), None, "cell", None),
            P(),
            P("groups", None),
            P(("groups", "cell"), None),
            P(("groups", "cell")),
            P(("groups", "cell"), None),
            P(("groups", "cell"), None),
        ),
        out_specs=P(("groups", "member"), None, "cell", None),
        check_vma=False,
    )
```

```python
import functools

import jax
import jax.numpy as jnp
from jax import lax
from jax.experimental import pallas as pl
from jax.experimental.pallas import tpu as pltpu
from jax.sharding import PartitionSpec as P

SUBSTEPS = 4
BAND = 4
ROOT_STEPS = 24
HALO = SUBSTEPS
DIFFUSION = 0.02
MESH = pl.DeviceIdType.MESH
HIGHEST = lax.Precision.HIGHEST
VMEM_LIMIT = 48 * 1024 * 1024


def stencil_coeffs(regimes, wind_table, first_row, tile_rows, row_total):
    row_ids = first_row - HALO + jnp.arange(tile_rows + 2 * HALO)
    band_ids = jnp.clip(row_ids, 0, row_total - 1) // BAND
    band_hits = band_ids[:, None, None] == jnp.arange(regimes.shape[0])[None, :, None]
    ids = jnp.sum(jnp.where(band_hits, regimes[None], 0), axis=1)
    hits = ids[:, :, None, None] == jnp.arange(wind_table.shape[0])[None, None, :, None]
    speed = jnp.sum(jnp.where(hits, wind_table[None, None], 0.0), axis=2)
    cx, cy = speed[:, :, 0], speed[:, :, 1]
    parts = [
        1.0 - jnp.abs(cx) - jnp.abs(cy) - 4.0 * DIFFUSION,
        jnp.maximum(cx, 0.0) + DIFFUSION,
        DIFFUSION - jnp.minimum(cx, 0.0),
        jnp.maximum(cy, 0.0) + DIFFUSION,
        DIFFUSION - jnp.minimum(cy, 0.0),
    ]
    inside = (row_ids >= 0) & (row_ids < row_total)
    table = jnp.where(inside[:, None, None], jnp.stack(parts, axis=2), 0.0)
    return table.reshape(row_ids.shape[0], SUBSTEPS * 5).T


def stencil_kernel(
    n_cell,
    chunk,
    coeff_ref,
    index_ref,
    x_ref,
    out_ref,
    pred_ref,
    keep,
    edge_up,
    edge_down,
    south,
    north,
    send_up,
    recv_up,
    send_down,
    recv_down,
):
    cell = lax.axis_index("cell")
    fields, rows, members, width = x_ref.shape
    has_south, has_north = cell > 0, cell < n_cell - 1
    below = lax.rem(cell + n_cell - 1, n_cell)
    above = lax.rem(cell + 1, n_cell)

    barrier = pltpu.get_barrier_semaphore()

    @pl.when(has_south)
    def _():
        pl.semaphore_signal(barrier, inc=1, device_id={"cell": below}, device_id_type=MESH)

    @pl.when(has_north)
    def _():
        pl.semaphore_signal(barrier, inc=1, device_id={"cell": above}, device_id_type=MESH)

    for f in range(fields):
        edge_up[f] = x_ref[f, rows - HALO :].astype(jnp.bfloat16)
        edge_down[f] = x_ref[f, :HALO].astype(jnp.bfloat16)

    neighbours = jnp.where(has_south, 1, 0) + jnp.where(has_north, 1, 0)
    pl.semaphore_wait(barrier, neighbours)

    def upward(f):
        return pltpu.make_async_remote_copy(
            src_ref=edge_up.at[f],
            dst_ref=south.at[f],
            send_sem=send_up.at[f],
            recv_sem=recv_up.at[f],
            device_id={"cell": above},
            device_id_type=MESH,
        )

    def downward(f):
        return pltpu.make_async_remote_copy(
            src_ref=edge_down.at[f],
            dst_ref=north.at[f],
            send_sem=send_down.at[f],
            recv_sem=recv_down.at[f],
            device_id={"cell": below},
            device_id_type=MESH,
        )

    for f in range(fields):

        @pl.when(has_north)
        def _():
            upward(f).start()

        @pl.when(has_south)
        def _():
            downward(f).start()

    @pl.when(cell == 0)
    def _():
        south[...] = jnp.zeros_like(south)

    @pl.when(cell == n_cell - 1)
    def _():
        north[...] = jnp.zeros_like(north)

    lane = lax.broadcasted_iota(jnp.int32, (chunk, width), 1)
    slots = index_ref.shape[1]
    column = lax.broadcasted_iota(jnp.int32, (width, slots), 0)

    def one_field(f, outer):
        @pl.when(has_south)
        def _():
            upward(f).wait_recv()

        @pl.when(has_north)
        def _():
            downward(f).wait_recv()

        def one_chunk(step_at, carry):
            at = pl.ds(pl.multiple_of(step_at * chunk, chunk), chunk)
            cells = [south[f, i, at, :].astype(jnp.float32) for i in range(HALO)]
            cells += [x_ref[f, i, at, :] for i in range(rows)]
            cells += [north[f, i, at, :].astype(jnp.float32) for i in range(HALO)]
            for s in range(SUBSTEPS):
                fresh = list(cells)
                for i in range(s + 1, rows + 2 * HALO - s - 1):
                    q = cells[i]
                    west = jnp.where(lane == 0, 0.0, pltpu.roll(q, 1, 1))
                    east = jnp.where(lane == width - 1, 0.0, pltpu.roll(q, width - 1, 1))
                    fresh[i] = (
                        q * coeff_ref[s * 5, i]
                        + cells[i - 1] * coeff_ref[s * 5 + 1, i]
                        + cells[i + 1] * coeff_ref[s * 5 + 2, i]
                        + west * coeff_ref[s * 5 + 3, i]
                        + east * coeff_ref[s * 5 + 4, i]
                    )
                cells = fresh
            for i in range(rows):
                out_ref[f, i, at, :] = cells[HALO + i].astype(jnp.bfloat16)
                keep[i, at, :] = cells[HALO + i]
            return carry

        lax.fori_loop(0, members // chunk, one_chunk, 0)

        @pl.when(f == 0)
        def _():
            pred_ref[...] = jnp.zeros_like(pred_ref)

            def one_row(i, carry):
                hits = jnp.where(column == index_ref[...] - i * width, 1.0, 0.0)
                picked = jnp.dot(
                    jnp.concatenate(split3(keep[i]), axis=0),
                    hits.astype(jnp.bfloat16),
                    preferred_element_type=jnp.float32,
                )
                pred_ref[...] += (
                    picked[:members] + picked[members : 2 * members] + picked[2 * members :]
                )
                return carry

            lax.fori_loop(0, rows, one_row, 0)

        return outer

    lax.fori_loop(0, fields, one_field, 0)

    for f in range(fields):

        @pl.when(has_north)
        def _():
            upward(f).wait_send()

        @pl.when(has_south)
        def _():
            downward(f).wait_send()


def stencil_call(coeffs, obs_index, cells):
    fields, rows, members, width = cells.shape
    vmem = pl.BlockSpec(memory_space=pltpu.VMEM)
    edge = pltpu.VMEM((fields, HALO, members, width), jnp.bfloat16)
    return pl.pallas_call(
        functools.partial(stencil_kernel, lax.axis_size("cell"), 16),
        in_specs=[pl.BlockSpec(memory_space=pltpu.SMEM), vmem, vmem],
        out_specs=[vmem, vmem],
        out_shape=[
            jax.ShapeDtypeStruct(cells.shape, jnp.bfloat16),
            jax.ShapeDtypeStruct((members, obs_index.shape[1]), jnp.float32),
        ],
        scratch_shapes=[pltpu.VMEM((rows, members, width), jnp.float32)]
        + [edge] * 4
        + [pltpu.SemaphoreType.DMA((fields,))] * 4,
        compiler_params=pltpu.CompilerParams(
            collective_id=1, has_side_effects=True, vmem_limit_bytes=VMEM_LIMIT
        ),
    )(coeffs, obs_index, cells)


def split3(x):
    high = x.astype(jnp.bfloat16)
    rest = x - high.astype(jnp.float32)
    middle = rest.astype(jnp.bfloat16)
    return high, middle, (rest - middle.astype(jnp.float32)).astype(jnp.bfloat16)


def six_products(a, b):
    left = jnp.concatenate([a[2], a[1], a[0], a[1], a[0], a[0]], axis=1)
    right = jnp.concatenate([b[0], b[1], b[2], b[0], b[1], b[0]], axis=0)
    return jnp.dot(left, right, preferred_element_type=jnp.float32)


def nt_dot(a, b):
    return lax.dot_general(
        a, b, (((1,), (1,)), ((), ())), precision=HIGHEST, preferred_element_type=jnp.float32
    )


def nn_dot(a, b):
    return jnp.dot(a, b, precision=HIGHEST, preferred_element_type=jnp.float32)


def analysis_kernel(
    n_cell,
    n_member,
    pred_ref,
    weight_ref,
    value_ref,
    forecast_ref,
    out_ref,
    pieces,
    coeff,
    everyone,
    mine,
    others,
    total,
    gram,
    upper,
    lower,
    send_pred,
    recv_pred,
    send_part,
    recv_part,
    send_gram,
    recv_gram,
    send_far,
    recv_far,
    send_mate,
    recv_mate,
):
    cell = lax.axis_index("cell")
    member = lax.axis_index("member")
    count = pred_ref.shape[0]
    members = count * n_member

    barrier = pltpu.get_barrier_semaphore()
    for d in range(1, n_member):
        pl.semaphore_signal(
            barrier, inc=1, device_id={"member": lax.rem(member + d, n_member)}, device_id_type=MESH
        )
    for d in range(1, n_cell):
        pl.semaphore_signal(
            barrier, inc=1, device_id={"cell": lax.rem(cell + d, n_cell)}, device_id_type=MESH
        )
    pl.semaphore_wait(barrier, n_member + n_cell - 2)

    own = pl.ds(pl.multiple_of(member * count, count), count)
    fields, rows_here = forecast_ref.shape[:2]
    chips = n_member // 2
    mate = member + 1 - 2 * lax.rem(member, 2)

    def to_far(d, f):
        return pltpu.make_async_remote_copy(
            src_ref=forecast_ref.at[f],
            dst_ref=pieces.at[member, f],
            send_sem=send_far.at[d, f],
            recv_sem=recv_far.at[d, f],
            device_id={"member": lax.rem(member + 2 * d, n_member)},
            device_id_type=MESH,
        )

    def to_mate(d, f):
        owner = lax.rem(member + n_member - 2 * d, n_member)
        return pltpu.make_async_remote_copy(
            src_ref=forecast_ref.at[f] if d == 0 else pieces.at[owner, f],
            dst_ref=pieces.at[owner, f],
            send_sem=send_mate.at[d, f],
            recv_sem=recv_mate.at[d, f],
            device_id={"member": mate},
            device_id_type=MESH,
        )

    def send_field(f):
        for d in range(1, chips):
            to_far(d, f).start()
        to_mate(0, f).start()

    def forward_field(f):
        for d in range(1, chips):
            to_far(d, f).wait_recv()
            to_mate(d, f).start()

    copies = []
    for d in range(1, n_member):
        copy = pltpu.make_async_remote_copy(
            src_ref=pred_ref,
            dst_ref=everyone.at[own],
            send_sem=send_pred.at[d],
            recv_sem=recv_pred.at[d],
            device_id={"member": lax.rem(member + d, n_member)},
            device_id_type=MESH,
        )
        copy.start()
        copies.append(copy)
    everyone[own, :] = pred_ref[...]
    for copy in copies:
        copy.wait()

    send_field(0)
    predicted = everyone[...]
    ybar = jnp.mean(predicted, axis=0, keepdims=True)
    weight = weight_ref[...]
    scaled = (predicted - ybar) * weight
    local = (pred_ref[...] - ybar) * weight
    innovation = jnp.broadcast_to(weight * (value_ref[...] - ybar), (8, weight.shape[1]))
    mine[...] = nt_dot(jnp.concatenate([local, innovation], axis=0), scaled)

    copies = []
    for d in range(1, n_cell):
        copy = pltpu.make_async_remote_copy(
            src_ref=mine,
            dst_ref=others.at[d - 1],
            send_sem=send_part.at[d],
            recv_sem=recv_part.at[d],
            device_id={"cell": lax.rem(cell + d, n_cell)},
            device_id_type=MESH,
        )
        copy.start()
        copies.append(copy)
    for copy in copies:
        copy.wait()
    summed = mine[...]
    for d in range(n_cell - 1):
        summed = summed + others[d]
    total[...] = summed

    copies = []
    for d in range(1, n_member):
        copy = pltpu.make_async_remote_copy(
            src_ref=total.at[pl.ds(0, count)],
            dst_ref=gram.at[own],
            send_sem=send_gram.at[d],
            recv_sem=recv_gram.at[d],
            device_id={"member": lax.rem(member + d, n_member)},
            device_id_type=MESH,
        )
        copy.start()
        copies.append(copy)
    gram[own, :] = total[pl.ds(0, count), :]
    for copy in copies:
        copy.wait()

    for f in range(1, fields):
        send_field(f)
    pieces[member] = forecast_ref[...]

    rows = lax.broadcasted_iota(jnp.int32, (members, members), 0)
    columns = lax.broadcasted_iota(jnp.int32, (members, members), 1)
    identity = jnp.where(rows == columns, 1.0, 0.0).astype(jnp.float32)
    precision = gram[...] + (members - 1.0) * identity
    scale = jnp.sum(jnp.sum(precision * identity, axis=1, keepdims=True), axis=0, keepdims=True)
    upper[...] = precision / scale
    lower[...] = identity

    def newton(step, carry):
        y, z = split3(upper[...]), split3(lower[...])
        middle = split3(1.5 * identity - 0.5 * six_products(z, y))
        upper[...] = six_products(y, middle)
        lower[...] = six_products(middle, z)
        return carry

    for f in range(fields):
        lax.fori_loop(ROOT_STEPS * f // fields, ROOT_STEPS * (f + 1) // fields, newton, 0)
        forward_field(f)

    gain = total[pl.ds(count, 8), :]
    half_way = nt_dot(gain, lower[...])
    mean_weights = nt_dot(half_way, lower[...])[0:1, :] / scale
    root = jnp.sqrt((members - 1.0) / scale) * lower[own, :]
    blend = mean_weights + root
    transform = blend - jnp.mean(blend, axis=1, keepdims=True) + 1.0 / members
    coeff[...] = transform.astype(jnp.bfloat16)

    for f in range(fields):
        for d in range(chips):
            to_mate(d, f).wait()
        for d in range(1, chips):
            to_far(d, f).wait_send()

        def blend_row(r, carry):
            block = pieces[:, f, r].reshape(members, pieces.shape[4])
            out_ref[f, r] = jnp.dot(coeff[...], block, preferred_element_type=jnp.float32)
            return carry

        lax.fori_loop(0, rows_here, blend_row, 0)


def analysis_call(local_pred, weight, value, forecast):
    n_cell, n_member = lax.axis_size("cell"), lax.axis_size("member")
    count, slots = local_pred.shape
    members = count * n_member
    fields = forecast.shape[0]
    vmem = pl.BlockSpec(memory_space=pltpu.VMEM)
    dma = pltpu.SemaphoreType.DMA
    return pl.pallas_call(
        functools.partial(analysis_kernel, n_cell, n_member),
        out_shape=jax.ShapeDtypeStruct(forecast.shape, jnp.float32),
        in_specs=[vmem] * 4,
        out_specs=vmem,
        scratch_shapes=[
            pltpu.VMEM((n_member,) + forecast.shape, jnp.bfloat16),
            pltpu.VMEM((count, members), jnp.bfloat16),
            pltpu.VMEM((members, slots), jnp.float32),
            pltpu.VMEM((count + 8, members), jnp.float32),
            pltpu.VMEM((n_cell - 1, count + 8, members), jnp.float32),
            pltpu.VMEM((count + 8, members), jnp.float32),
            pltpu.VMEM((members, members), jnp.float32),
            pltpu.VMEM((members, members), jnp.float32),
            pltpu.VMEM((members, members), jnp.float32),
            dma((n_member,)),
            dma((n_member,)),
            dma((n_cell,)),
            dma((n_cell,)),
            dma((n_member,)),
            dma((n_member,)),
        ]
        + [dma((n_member // 2, fields))] * 4,
        compiler_params=pltpu.CompilerParams(
            collective_id=0, has_side_effects=True, vmem_limit_bytes=VMEM_LIMIT
        ),
    )(local_pred, weight, value, forecast)


def shards(prior_sample_set, wind_table, regimes, obs_index, obs_count, obs_value, obs_var):
    tile_rows = prior_sample_set.shape[2]
    row_total = tile_rows * lax.axis_size("cell")
    first_row = lax.axis_index("cell") * tile_rows
    coeffs = stencil_coeffs(regimes, wind_table, first_row, tile_rows, row_total)
    live = jnp.arange(obs_var.shape[1])[None, :] < obs_count[0]
    weight = live.astype(jnp.float32) / jnp.sqrt(obs_var)

    cells = prior_sample_set.transpose(1, 2, 0, 3)
    forecast, local_pred = stencil_call(coeffs, obs_index, cells)
    blended = analysis_call(local_pred, weight, obs_value, forecast)
    return blended.transpose(2, 0, 1, 3)


def solution(mesh):
    return jax.shard_map(
        shards,
        mesh=mesh,
        in_specs=(
            P(("groups", "member"), None, "cell", None),
            P(),
            P("groups", None),
            P(("groups", "cell"), None),
            P(("groups", "cell")),
            P(("groups", "cell"), None),
            P(("groups", "cell"), None),
        ),
        out_specs=P(("groups", "member"), None, "cell", None),
        check_vma=False,
    )
```

```python
import functools

import jax
import jax.numpy as jnp
from jax import lax
from jax.experimental import pallas as pl
from jax.experimental.pallas import tpu as pltpu
from jax.sharding import PartitionSpec as P

SUBSTEPS = 4
BAND = 4
ROOT_STEPS = 24
HALO = SUBSTEPS
DIFFUSION = 0.02
MESH = pl.DeviceIdType.MESH
HIGHEST = lax.Precision.HIGHEST
VMEM_LIMIT = 56 * 1024 * 1024
CHUNK = 16


def split3(x):
    high = x.astype(jnp.bfloat16)
    rest = x - high.astype(jnp.float32)
    middle = rest.astype(jnp.bfloat16)
    return high, middle, (rest - middle.astype(jnp.float32)).astype(jnp.bfloat16)


def six_products(a, b):
    left = jnp.concatenate([a[2], a[1], a[0], a[1], a[0], a[0]], axis=1)
    right = jnp.concatenate([b[0], b[1], b[2], b[0], b[1], b[0]], axis=0)
    return jnp.dot(left, right, preferred_element_type=jnp.float32)


def nt_dot(a, b):
    return lax.dot_general(
        a, b, (((1,), (1,)), ((), ())), precision=HIGHEST, preferred_element_type=jnp.float32
    )


def nn_dot(a, b):
    return jnp.dot(a, b, precision=HIGHEST, preferred_element_type=jnp.float32)


def cycle_kernel(
    n_cell,
    n_member,
    regime_ref,
    wind_ref,
    count_ref,
    index_ref,
    value_ref,
    var_ref,
    x_ref,
    out_ref,
    table,
    keep,
    edge_up,
    edge_down,
    south,
    north,
    forecast,
    pieces,
    pred,
    coeff,
    everyone,
    mine,
    others,
    total,
    gram,
    upper,
    lower,
    send_up,
    recv_up,
    send_down,
    recv_down,
    send_pred,
    recv_pred,
    send_part,
    recv_part,
    send_gram,
    recv_gram,
    send_far,
    recv_far,
    send_mate,
    recv_mate,
):
    cell = lax.axis_index("cell")
    member = lax.axis_index("member")
    fields, rows, count, width = x_ref.shape
    slots = index_ref.shape[1]
    members = count * n_member
    chips = n_member // 2
    mate = member + 1 - 2 * lax.rem(member, 2)
    own = pl.ds(pl.multiple_of(member * count, count), count)
    has_south, has_north = cell > 0, cell < n_cell - 1

    barrier = pltpu.get_barrier_semaphore()
    for d in range(1, n_member):
        pl.semaphore_signal(
            barrier, inc=1, device_id={"member": lax.rem(member + d, n_member)}, device_id_type=MESH
        )
    for d in range(1, n_cell):
        pl.semaphore_signal(
            barrier, inc=1, device_id={"cell": lax.rem(cell + d, n_cell)}, device_id_type=MESH
        )

    def remote(src, dst, send, recv, **device):
        return pltpu.make_async_remote_copy(
            src_ref=src,
            dst_ref=dst,
            send_sem=send,
            recv_sem=recv,
            device_id=device,
            device_id_type=MESH,
        )

    def upward(f):
        above = lax.rem(cell + 1, n_cell)
        return remote(edge_up.at[f], south.at[f], send_up.at[f], recv_up.at[f], cell=above)

    def downward(f):
        below = lax.rem(cell + n_cell - 1, n_cell)
        return remote(edge_down.at[f], north.at[f], send_down.at[f], recv_down.at[f], cell=below)

    def to_far(d, f):
        return remote(
            forecast.at[f],
            pieces.at[member, f],
            send_far.at[d, f],
            recv_far.at[d, f],
            member=lax.rem(member + 2 * d, n_member),
        )

    def to_mate(d, f):
        owner = lax.rem(member + n_member - 2 * d, n_member)
        return remote(
            forecast.at[f] if d == 0 else pieces.at[owner, f],
            pieces.at[owner, f],
            send_mate.at[d, f],
            recv_mate.at[d, f],
            member=mate,
        )

    def send_field(f):
        for d in range(1, chips):
            to_far(d, f).start()
        to_mate(0, f).start()

    def forward_field(f):
        for d in range(1, chips):
            to_far(d, f).wait_recv()
            to_mate(d, f).start()

    def cast_edges(f):
        for i in range(HALO):
            edge_up[f, i] = x_ref[f, rows - HALO + i].astype(jnp.bfloat16)
            edge_down[f, i] = x_ref[f, i].astype(jnp.bfloat16)

    def send_edges(f):
        @pl.when(has_north)
        def _():
            upward(f).start()

        @pl.when(has_south)
        def _():
            downward(f).start()

    cast_edges(0)
    pl.semaphore_wait(barrier, n_member + n_cell - 2)
    send_edges(0)
    for f in range(1, fields):
        cast_edges(f)
        send_edges(f)

    @pl.when(cell == 0)
    def _():
        south[...] = jnp.zeros_like(south)

    @pl.when(cell == n_cell - 1)
    def _():
        north[...] = jnp.zeros_like(north)

    row_total = rows * n_cell

    def one_table_row(i, carry):
        row = cell * rows + i - HALO
        inside = jnp.where((row >= 0) & (row < row_total), 1.0, 0.0)
        band = jnp.minimum(jnp.maximum(row, 0), row_total - 1) // BAND
        for s in range(SUBSTEPS):
            regime = regime_ref[band, s]
            cx, cy = wind_ref[regime, 0], wind_ref[regime, 1]
            x_up, x_down = jnp.maximum(cx, 0.0), jnp.minimum(cx, 0.0)
            y_up, y_down = jnp.maximum(cy, 0.0), jnp.minimum(cy, 0.0)
            table[s * 5, i] = inside * (1.0 - 4.0 * DIFFUSION - x_up + x_down - y_up + y_down)
            table[s * 5 + 1, i] = inside * (x_up + DIFFUSION)
            table[s * 5 + 2, i] = inside * (DIFFUSION - x_down)
            table[s * 5 + 3, i] = inside * (y_up + DIFFUSION)
            table[s * 5 + 4, i] = inside * (DIFFUSION - y_down)
        return carry

    lax.fori_loop(0, rows + 2 * HALO, one_table_row, 0)

    lane = lax.broadcasted_iota(jnp.int32, (CHUNK, width), 1)

    def stencil(f):
        @pl.when(has_south)
        def _():
            upward(f).wait_recv()

        @pl.when(has_north)
        def _():
            downward(f).wait_recv()

        def one_chunk(step_at, carry):
            at = pl.ds(pl.multiple_of(step_at * CHUNK, CHUNK), CHUNK)
            cells = [south[f, i, at, :].astype(jnp.float32) for i in range(HALO)]
            cells += [x_ref[f, i, at, :] for i in range(rows)]
            cells += [north[f, i, at, :].astype(jnp.float32) for i in range(HALO)]
            for s in range(SUBSTEPS):
                fresh = list(cells)
                for i in range(s + 1, rows + 2 * HALO - s - 1):
                    q = cells[i]
                    west = jnp.where(lane == 0, 0.0, pltpu.roll(q, 1, 1))
                    east = jnp.where(lane == width - 1, 0.0, pltpu.roll(q, width - 1, 1))
                    fresh[i] = (
                        q * table[s * 5, i]
                        + cells[i - 1] * table[s * 5 + 1, i]
                        + cells[i + 1] * table[s * 5 + 2, i]
                        + west * table[s * 5 + 3, i]
                        + east * table[s * 5 + 4, i]
                    )
                cells = fresh
            for i in range(rows):
                forecast[f, i, at, :] = cells[HALO + i].astype(jnp.bfloat16)
                if f == 0:
                    keep[i, at, :] = cells[HALO + i]
            return carry

        lax.fori_loop(0, count // CHUNK, one_chunk, 0)

    stencil(0)
    column = lax.broadcasted_iota(jnp.int32, (width, slots), 0)
    pred[...] = jnp.zeros_like(pred)

    def pick_row(i, carry):
        hits = jnp.where(column == index_ref[...] - i * width, 1.0, 0.0)
        picked = jnp.dot(
            jnp.concatenate(split3(keep[i]), axis=0),
            hits.astype(jnp.bfloat16),
            preferred_element_type=jnp.float32,
        )
        pred[...] += picked[:count] + picked[count : 2 * count] + picked[2 * count :]
        return carry

    lax.fori_loop(0, rows, pick_row, 0)

    def share_pred(d):
        peer = lax.rem(member + d, n_member)
        return remote(pred, everyone.at[own], send_pred.at[d], recv_pred.at[d], member=peer)

    def share_part(d):
        peer = lax.rem(cell + d, n_cell)
        return remote(mine, others.at[d - 1], send_part.at[d], recv_part.at[d], cell=peer)

    def share_gram(d):
        peer = lax.rem(member + d, n_member)
        src = total.at[pl.ds(0, count)]
        return remote(src, gram.at[own], send_gram.at[d], recv_gram.at[d], member=peer)

    for d in range(1, n_member):
        share_pred(d).start()
    everyone[own, :] = pred[...]
    send_field(0)
    if fields > 1:
        stencil(1)
    for d in range(1, n_member):
        share_pred(d).wait()

    predicted = everyone[...]
    ybar = jnp.mean(predicted, axis=0, keepdims=True)
    live = lax.broadcasted_iota(jnp.int32, (1, slots), 1) < count_ref[0]
    weight = jnp.where(live, 1.0, 0.0) / jnp.sqrt(var_ref[...])
    scaled = (predicted - ybar) * weight
    local = (pred[...] - ybar) * weight
    innovation = jnp.broadcast_to(weight * (value_ref[...] - ybar), (8, slots))
    mine[...] = nt_dot(jnp.concatenate([local, innovation], axis=0), scaled)
    for d in range(1, n_cell):
        share_part(d).start()
    for f in range(2, fields):
        stencil(f)
    for d in range(1, n_cell):
        share_part(d).wait()
    summed = mine[...]
    for d in range(n_cell - 1):
        summed = summed + others[d]
    total[...] = summed
    for d in range(1, n_member):
        share_gram(d).start()
    for f in range(1, fields):
        send_field(f)
    gram[own, :] = total[pl.ds(0, count), :]
    pieces[member] = forecast[...]
    for d in range(1, n_member):
        share_gram(d).wait()

    lines = lax.broadcasted_iota(jnp.int32, (members, members), 0)
    columns = lax.broadcasted_iota(jnp.int32, (members, members), 1)
    identity = jnp.where(lines == columns, 1.0, 0.0).astype(jnp.float32)
    precision = gram[...] + (members - 1.0) * identity
    scale = jnp.sum(jnp.sum(precision * identity, axis=1, keepdims=True), axis=0, keepdims=True)
    upper[...] = precision / scale
    lower[...] = identity

    def newton(step, carry):
        y, z = split3(upper[...]), split3(lower[...])
        middle = split3(1.5 * identity - 0.5 * six_products(z, y))
        upper[...] = six_products(y, middle)
        lower[...] = six_products(middle, z)
        return carry

    for f in range(fields):
        lax.fori_loop(ROOT_STEPS * f // fields, ROOT_STEPS * (f + 1) // fields, newton, 0)
        forward_field(f)

    gain = total[pl.ds(count, 8), :]
    half_way = nt_dot(gain, lower[...])
    mean_weights = nt_dot(half_way, lower[...])[0:1, :] / scale
    root = jnp.sqrt((members - 1.0) / scale) * lower[own, :]
    blend = mean_weights + root
    transform = blend - jnp.mean(blend, axis=1, keepdims=True) + 1.0 / members
    coeff[...] = transform.astype(jnp.bfloat16)

    for f in range(fields):
        for d in range(chips):
            to_mate(d, f).wait()
        for d in range(1, chips):
            to_far(d, f).wait_send()

        def blend_row(r, carry):
            block = pieces[:, f, r].reshape(members, width)
            out_ref[f, r] = jnp.dot(coeff[...], block, preferred_element_type=jnp.float32)
            return carry

        lax.fori_loop(0, rows, blend_row, 0)

    for f in range(fields):

        @pl.when(has_north)
        def _():
            upward(f).wait_send()

        @pl.when(has_south)
        def _():
            downward(f).wait_send()


def shards(prior_sample_set, wind_table, regimes, obs_index, obs_count, obs_value, obs_var):
    n_cell, n_member = lax.axis_size("cell"), lax.axis_size("member")
    count, fields, rows, width = prior_sample_set.shape
    slots = obs_index.shape[1]
    members = count * n_member
    cells = prior_sample_set.transpose(1, 2, 0, 3)
    smem = pl.BlockSpec(memory_space=pltpu.SMEM)
    vmem = pl.BlockSpec(memory_space=pltpu.VMEM)
    single, half = jnp.float32, jnp.bfloat16
    edge = pltpu.VMEM((fields, HALO, count, width), half)
    square = pltpu.VMEM((members, members), single)
    part = (count + 8, members)
    dma = pltpu.SemaphoreType.DMA
    blended = pl.pallas_call(
        functools.partial(cycle_kernel, n_cell, n_member),
        in_specs=[smem] * 3 + [vmem] * 4,
        out_specs=vmem,
        out_shape=jax.ShapeDtypeStruct(cells.shape, single),
        scratch_shapes=[
            pltpu.SMEM((SUBSTEPS * 5, rows + 2 * HALO), single),
            pltpu.VMEM((rows, count, width), single),
            edge,
            edge,
            edge,
            edge,
            pltpu.VMEM((fields, rows, count, width), half),
            pltpu.VMEM((n_member, fields, rows, count, width), half),
            pltpu.VMEM((count, slots), single),
            pltpu.VMEM((count, members), half),
            pltpu.VMEM((members, slots), single),
            pltpu.VMEM(part, single),
            pltpu.VMEM((n_cell - 1,) + part, single),
            pltpu.VMEM(part, single),
            square,
            square,
            square,
        ]
        + [dma((fields,))] * 4
        + [dma((n_member,))] * 2
        + [dma((n_cell,))] * 2
        + [dma((n_member,))] * 2
        + [dma((n_member // 2, fields))] * 4,
        compiler_params=pltpu.CompilerParams(
            collective_id=0, has_side_effects=True, vmem_limit_bytes=VMEM_LIMIT
        ),
    )(regimes, wind_table, obs_count, obs_index, obs_value, obs_var, cells)
    return blended.transpose(2, 0, 1, 3)


def solution(mesh):
    return jax.shard_map(
        shards,
        mesh=mesh,
        in_specs=(
            P(("groups", "member"), None, "cell", None),
            P(),
            P("groups", None),
            P(("groups", "cell"), None),
            P(("groups", "cell")),
            P(("groups", "cell"), None),
            P(("groups", "cell"), None),
        ),
        out_specs=P(("groups", "member"), None, "cell", None),
        check_vma=False,
    )
```

```python
import functools

import jax
import jax.numpy as jnp
from jax import lax
from jax.experimental import pallas as pl
from jax.experimental.pallas import tpu as pltpu
from jax.sharding import PartitionSpec as P

SUBSTEPS = 4
BAND = 4
ROOT_STEPS = 24
HALO = SUBSTEPS
DIFFUSION = 0.02
MESH = pl.DeviceIdType.MESH
HIGHEST = lax.Precision.HIGHEST
VMEM_LIMIT = 26 * 1024 * 1024
CHUNK = 16


def split3(x):
    high = x.astype(jnp.bfloat16)
    rest = x - high.astype(jnp.float32)
    middle = rest.astype(jnp.bfloat16)
    return high, middle, (rest - middle.astype(jnp.float32)).astype(jnp.bfloat16)


def six_products(a, b):
    left = jnp.concatenate([a[2], a[1], a[0], a[1], a[0], a[0]], axis=1)
    right = jnp.concatenate([b[0], b[1], b[2], b[0], b[1], b[0]], axis=0)
    return jnp.dot(left, right, preferred_element_type=jnp.float32)


def nt_dot(a, b):
    return lax.dot_general(
        a, b, (((1,), (1,)), ((), ())), precision=HIGHEST, preferred_element_type=jnp.float32
    )


def nn_dot(a, b):
    return jnp.dot(a, b, precision=HIGHEST, preferred_element_type=jnp.float32)


def cycle_kernel(
    n_cell,
    n_member,
    regime_ref,
    wind_ref,
    count_ref,
    index_ref,
    value_ref,
    var_ref,
    x_ref,
    out_ref,
    table,
    keep,
    edge_up,
    edge_down,
    south,
    north,
    pieces,
    pred,
    coeff,
    everyone,
    mine,
    others,
    total,
    gram,
    upper,
    lower,
    send_up,
    recv_up,
    send_down,
    recv_down,
    send_pred,
    recv_pred,
    send_part,
    recv_part,
    send_gram,
    recv_gram,
    send_far,
    recv_far,
    send_mate,
    recv_mate,
):
    cell = lax.axis_index("cell")
    member = lax.axis_index("member")
    fields, rows, count, width = x_ref.shape
    slots = index_ref.shape[1]
    members = count * n_member
    chips = n_member // 2
    mate = member + 1 - 2 * lax.rem(member, 2)
    own = pl.ds(pl.multiple_of(member * count, count), count)
    has_south, has_north = cell > 0, cell < n_cell - 1

    barrier = pltpu.get_barrier_semaphore()
    for d in range(1, n_member):
        pl.semaphore_signal(
            barrier, inc=1, device_id={"member": lax.rem(member + d, n_member)}, device_id_type=MESH
        )
    for d in range(1, n_cell):
        pl.semaphore_signal(
            barrier, inc=1, device_id={"cell": lax.rem(cell + d, n_cell)}, device_id_type=MESH
        )

    def remote(src, dst, send, recv, **device):
        return pltpu.make_async_remote_copy(
            src_ref=src,
            dst_ref=dst,
            send_sem=send,
            recv_sem=recv,
            device_id=device,
            device_id_type=MESH,
        )

    def upward(f):
        above = lax.rem(cell + 1, n_cell)
        return remote(edge_up.at[f], south.at[f], send_up.at[f], recv_up.at[f], cell=above)

    def downward(f):
        below = lax.rem(cell + n_cell - 1, n_cell)
        return remote(edge_down.at[f], north.at[f], send_down.at[f], recv_down.at[f], cell=below)

    def to_far(d, f):
        return remote(
            pieces.at[member, f],
            pieces.at[member, f],
            send_far.at[d, f],
            recv_far.at[d, f],
            member=lax.rem(member + 2 * d, n_member),
        )

    def to_mate(d, f):
        owner = lax.rem(member + n_member - 2 * d, n_member)
        return remote(
            pieces.at[owner, f],
            pieces.at[owner, f],
            send_mate.at[d, f],
            recv_mate.at[d, f],
            member=mate,
        )

    def send_field(f):
        for d in range(1, chips):
            to_far(d, f).start()
        to_mate(0, f).start()

    def forward_field(f):
        for d in range(1, chips):
            to_far(d, f).wait_recv()
            to_mate(d, f).start()

    def cast_edges(f):
        for i in range(HALO):
            edge_up[f, i] = x_ref[f, rows - HALO + i].astype(jnp.bfloat16)
            edge_down[f, i] = x_ref[f, i].astype(jnp.bfloat16)

    def send_edges(f):
        @pl.when(has_north)
        def _():
            upward(f).start()

        @pl.when(has_south)
        def _():
            downward(f).start()

    cast_edges(0)
    pl.semaphore_wait(barrier, n_member + n_cell - 2)
    send_edges(0)
    for f in range(1, fields):
        cast_edges(f)
        send_edges(f)

    @pl.when(cell == 0)
    def _():
        south[...] = jnp.zeros_like(south)

    @pl.when(cell == n_cell - 1)
    def _():
        north[...] = jnp.zeros_like(north)

    row_total = rows * n_cell

    def one_table_row(i, carry):
        row = cell * rows + i - HALO
        inside = jnp.where((row >= 0) & (row < row_total), 1.0, 0.0)
        band = jnp.minimum(jnp.maximum(row, 0), row_total - 1) // BAND
        for s in range(SUBSTEPS):
            regime = regime_ref[s, band]
            cx, cy = wind_ref[0, regime], wind_ref[1, regime]
            x_up, x_down = jnp.maximum(cx, 0.0), jnp.minimum(cx, 0.0)
            y_up, y_down = jnp.maximum(cy, 0.0), jnp.minimum(cy, 0.0)
            table[s * 5, i] = inside * (1.0 - 4.0 * DIFFUSION - x_up + x_down - y_up + y_down)
            table[s * 5 + 1, i] = inside * (x_up + DIFFUSION)
            table[s * 5 + 2, i] = inside * (DIFFUSION - x_down)
            table[s * 5 + 3, i] = inside * (y_up + DIFFUSION)
            table[s * 5 + 4, i] = inside * (DIFFUSION - y_down)
        return carry

    lax.fori_loop(0, rows + 2 * HALO, one_table_row, 0)

    lane = lax.broadcasted_iota(jnp.int32, (CHUNK, width), 1)

    def stencil(f):
        @pl.when(has_south)
        def _():
            upward(f).wait_recv()

        @pl.when(has_north)
        def _():
            downward(f).wait_recv()

        def one_chunk(step_at, carry):
            at = pl.ds(pl.multiple_of(step_at * CHUNK, CHUNK), CHUNK)
            cells = [south[f, i, at, :].astype(jnp.float32) for i in range(HALO)]
            cells += [x_ref[f, i, at, :] for i in range(rows)]
            cells += [north[f, i, at, :].astype(jnp.float32) for i in range(HALO)]
            for s in range(SUBSTEPS):
                fresh = list(cells)
                for i in range(s + 1, rows + 2 * HALO - s - 1):
                    q = cells[i]
                    west = jnp.where(lane == 0, 0.0, pltpu.roll(q, 1, 1))
                    east = jnp.where(lane == width - 1, 0.0, pltpu.roll(q, width - 1, 1))
                    fresh[i] = (
                        q * table[s * 5, i]
                        + cells[i - 1] * table[s * 5 + 1, i]
                        + cells[i + 1] * table[s * 5 + 2, i]
                        + west * table[s * 5 + 3, i]
                        + east * table[s * 5 + 4, i]
                    )
                cells = fresh
            for i in range(rows):
                pieces[member, f, i, at, :] = cells[HALO + i].astype(jnp.bfloat16)
                if f == 0:
                    keep[i, at, :] = cells[HALO + i]
            return carry

        lax.fori_loop(0, count // CHUNK, one_chunk, 0)

    stencil(0)
    column = lax.broadcasted_iota(jnp.int32, (width, slots), 0)
    pred[...] = jnp.zeros_like(pred)

    def pick_row(i, carry):
        hits = jnp.where(column == index_ref[...] - i * width, 1.0, 0.0)
        picked = jnp.dot(
            jnp.concatenate(split3(keep[i]), axis=0),
            hits.astype(jnp.bfloat16),
            preferred_element_type=jnp.float32,
        )
        pred[...] += picked[:count] + picked[count : 2 * count] + picked[2 * count :]
        return carry

    lax.fori_loop(0, rows, pick_row, 0)

    def share_pred(d):
        peer = lax.rem(member + d, n_member)
        return remote(pred, everyone.at[own], send_pred.at[d], recv_pred.at[d], member=peer)

    def share_part(d):
        peer = lax.rem(cell + d, n_cell)
        return remote(mine, others.at[d - 1], send_part.at[d], recv_part.at[d], cell=peer)

    def share_gram(d):
        peer = lax.rem(member + d, n_member)
        src = total.at[pl.ds(0, count)]
        return remote(src, gram.at[own], send_gram.at[d], recv_gram.at[d], member=peer)

    for d in range(1, n_member):
        share_pred(d).start()
    everyone[own, :] = pred[...]
    send_field(0)
    if fields > 1:
        stencil(1)
    for d in range(1, n_member):
        share_pred(d).wait()

    predicted = everyone[...]
    ybar = jnp.mean(predicted, axis=0, keepdims=True)
    live = lax.broadcasted_iota(jnp.int32, (1, slots), 1) < count_ref[0]
    weight = jnp.where(live, 1.0, 0.0) / jnp.sqrt(var_ref[...])
    scaled = (predicted - ybar) * weight
    local = (pred[...] - ybar) * weight
    innovation = jnp.broadcast_to(weight * (value_ref[...] - ybar), (8, slots))
    mine[...] = nt_dot(jnp.concatenate([local, innovation], axis=0), scaled)
    for d in range(1, n_cell):
        share_part(d).start()
    for f in range(2, fields):
        stencil(f)
    for d in range(1, n_cell):
        share_part(d).wait()
    summed = mine[...]
    for d in range(n_cell - 1):
        summed = summed + others[d]
    total[...] = summed
    for d in range(1, n_member):
        share_gram(d).start()
    for f in range(1, fields):
        send_field(f)
    gram[own, :] = total[pl.ds(0, count), :]
    for d in range(1, n_member):
        share_gram(d).wait()

    lines = lax.broadcasted_iota(jnp.int32, (members, members), 0)
    columns = lax.broadcasted_iota(jnp.int32, (members, members), 1)
    identity = jnp.where(lines == columns, 1.0, 0.0).astype(jnp.float32)
    precision = gram[...] + (members - 1.0) * identity
    scale = jnp.sum(jnp.sum(precision * identity, axis=1, keepdims=True), axis=0, keepdims=True)
    upper[...] = precision / scale
    lower[...] = identity

    def newton(step, carry):
        y, z = split3(upper[...]), split3(lower[...])
        middle = split3(1.5 * identity - 0.5 * six_products(z, y))
        upper[...] = six_products(y, middle)
        lower[...] = six_products(middle, z)
        return carry

    for f in range(fields):
        lax.fori_loop(ROOT_STEPS * f // fields, ROOT_STEPS * (f + 1) // fields, newton, 0)
        forward_field(f)

    gain = total[pl.ds(count, 8), :]
    half_way = nt_dot(gain, lower[...])
    mean_weights = nt_dot(half_way, lower[...])[0:1, :] / scale
    root = jnp.sqrt((members - 1.0) / scale) * lower[own, :]
    blend = mean_weights + root
    transform = blend - jnp.mean(blend, axis=1, keepdims=True) + 1.0 / members
    coeff[...] = transform.astype(jnp.bfloat16)

    for f in range(fields):
        for d in range(chips):
            to_mate(d, f).wait()
        for d in range(1, chips):
            to_far(d, f).wait_send()

        def blend_row(r, carry):
            block = pieces[:, f, r].reshape(members, width)
            out_ref[f, r] = jnp.dot(coeff[...], block, preferred_element_type=jnp.float32)
            return carry

        lax.fori_loop(0, rows, blend_row, 0)

    for f in range(fields):

        @pl.when(has_north)
        def _():
            upward(f).wait_send()

        @pl.when(has_south)
        def _():
            downward(f).wait_send()


def shards(prior_sample_set, wind_table, regimes, obs_index, obs_count, obs_value, obs_var):
    n_cell, n_member = lax.axis_size("cell"), lax.axis_size("member")
    count, fields, rows, width = prior_sample_set.shape
    slots = obs_index.shape[1]
    members = count * n_member
    cells = prior_sample_set.transpose(1, 2, 0, 3)
    smem = pl.BlockSpec(memory_space=pltpu.SMEM)
    vmem = pl.BlockSpec(memory_space=pltpu.VMEM)
    single, half = jnp.float32, jnp.bfloat16
    edge = pltpu.VMEM((fields, HALO, count, width), half)
    square = pltpu.VMEM((members, members), single)
    part = (count + 8, members)
    dma = pltpu.SemaphoreType.DMA
    blended = pl.pallas_call(
        functools.partial(cycle_kernel, n_cell, n_member),
        in_specs=[smem] * 3 + [vmem] * 4,
        out_specs=vmem,
        out_shape=jax.ShapeDtypeStruct(cells.shape, single),
        scratch_shapes=[
            pltpu.SMEM((SUBSTEPS * 5, rows + 2 * HALO), single),
            pltpu.VMEM((rows, count, width), single),
            edge,
            edge,
            edge,
            edge,
            pltpu.VMEM((n_member, fields, rows, count, width), half),
            pltpu.VMEM((count, slots), single),
            pltpu.VMEM((count, members), half),
            pltpu.VMEM((members, slots), single),
            pltpu.VMEM(part, single),
            pltpu.VMEM((n_cell - 1,) + part, single),
            pltpu.VMEM(part, single),
            square,
            square,
            square,
        ]
        + [dma((fields,))] * 4
        + [dma((n_member,))] * 2
        + [dma((n_cell,))] * 2
        + [dma((n_member,))] * 2
        + [dma((n_member // 2, fields))] * 4,
        compiler_params=pltpu.CompilerParams(
            collective_id=0, has_side_effects=True, vmem_limit_bytes=VMEM_LIMIT
        ),
    )(regimes.T, wind_table.T, obs_count, obs_index, obs_value, obs_var, cells)
    return blended.transpose(2, 0, 1, 3)


def solution(mesh):
    return jax.shard_map(
        shards,
        mesh=mesh,
        in_specs=(
            P(("groups", "member"), None, "cell", None),
            P(),
            P("groups", None),
            P(("groups", "cell"), None),
            P(("groups", "cell")),
            P(("groups", "cell"), None),
            P(("groups", "cell"), None),
        ),
        out_specs=P(("groups", "member"), None, "cell", None),
        check_vma=False,
    )
```

```python
import functools

import jax
import jax.numpy as jnp
from jax import lax
from jax.experimental import pallas as pl
from jax.experimental.pallas import tpu as pltpu
from jax.sharding import PartitionSpec as P

SUBSTEPS = 4
BAND = 4
ROOT_STEPS = 24
HALO = SUBSTEPS
DIFFUSION = 0.02
MESH = pl.DeviceIdType.MESH
HIGHEST = lax.Precision.HIGHEST
VMEM_LIMIT = 30 * 1024 * 1024
CHUNK = 16


def split3(x):
    high = x.astype(jnp.bfloat16)
    rest = x - high.astype(jnp.float32)
    middle = rest.astype(jnp.bfloat16)
    return high, middle, (rest - middle.astype(jnp.float32)).astype(jnp.bfloat16)


def six_products(a, b):
    left = jnp.concatenate([a[2], a[1], a[0], a[1], a[0], a[0]], axis=1)
    right = jnp.concatenate([b[0], b[1], b[2], b[0], b[1], b[0]], axis=0)
    return jnp.dot(left, right, preferred_element_type=jnp.float32)


def nt_dot(a, b):
    return lax.dot_general(
        a, b, (((1,), (1,)), ((), ())), precision=HIGHEST, preferred_element_type=jnp.float32
    )


def nn_dot(a, b):
    return jnp.dot(a, b, precision=HIGHEST, preferred_element_type=jnp.float32)


def cycle_kernel(
    n_cell,
    n_member,
    regime_ref,
    wind_ref,
    count_ref,
    index_ref,
    value_ref,
    var_ref,
    x_ref,
    out_ref,
    table,
    hits,
    keep,
    edge_up,
    edge_down,
    south,
    north,
    pieces,
    pred,
    coeff,
    everyone,
    mine,
    others,
    total,
    gram,
    upper,
    lower,
    send_up,
    recv_up,
    send_down,
    recv_down,
    send_pred,
    recv_pred,
    send_part,
    recv_part,
    send_gram,
    recv_gram,
    send_far,
    recv_far,
    send_mate,
    recv_mate,
):
    cell = lax.axis_index("cell")
    member = lax.axis_index("member")
    fields, rows, count, width = x_ref.shape
    slots = index_ref.shape[1]
    members = count * n_member
    chips = n_member // 2
    mate = member + 1 - 2 * lax.rem(member, 2)
    own = pl.ds(pl.multiple_of(member * count, count), count)
    has_south, has_north = cell > 0, cell < n_cell - 1

    barrier = pltpu.get_barrier_semaphore()
    for d in range(1, n_member):
        pl.semaphore_signal(
            barrier, inc=1, device_id={"member": lax.rem(member + d, n_member)}, device_id_type=MESH
        )
    for d in range(1, n_cell):
        pl.semaphore_signal(
            barrier, inc=1, device_id={"cell": lax.rem(cell + d, n_cell)}, device_id_type=MESH
        )

    def remote(src, dst, send, recv, **device):
        return pltpu.make_async_remote_copy(
            src_ref=src,
            dst_ref=dst,
            send_sem=send,
            recv_sem=recv,
            device_id=device,
            device_id_type=MESH,
        )

    def upward(f):
        above = lax.rem(cell + 1, n_cell)
        return remote(edge_up.at[f], south.at[f], send_up.at[f], recv_up.at[f], cell=above)

    def downward(f):
        below = lax.rem(cell + n_cell - 1, n_cell)
        return remote(edge_down.at[f], north.at[f], send_down.at[f], recv_down.at[f], cell=below)

    def to_far(d, f):
        return remote(
            pieces.at[member, f],
            pieces.at[member, f],
            send_far.at[d, f],
            recv_far.at[d, f],
            member=lax.rem(member + 2 * d, n_member),
        )

    def to_mate(d, f):
        owner = lax.rem(member + n_member - 2 * d, n_member)
        return remote(
            pieces.at[owner, f],
            pieces.at[owner, f],
            send_mate.at[d, f],
            recv_mate.at[d, f],
            member=mate,
        )

    def send_field(f):
        for d in range(1, chips):
            to_far(d, f).start()
        to_mate(0, f).start()

    def forward_field(f):
        for d in range(1, chips):
            to_far(d, f).wait_recv()
            to_mate(d, f).start()

    def cast_edges(f):
        for i in range(HALO):
            edge_up[f, i] = x_ref[f, rows - HALO + i].astype(jnp.bfloat16)
            edge_down[f, i] = x_ref[f, i].astype(jnp.bfloat16)

    def send_edges(f):
        @pl.when(has_north)
        def _():
            upward(f).start()

        @pl.when(has_south)
        def _():
            downward(f).start()

    cast_edges(0)
    pl.semaphore_wait(barrier, n_member + n_cell - 2)
    send_edges(0)
    for f in range(1, fields):
        cast_edges(f)
        send_edges(f)

    @pl.when(cell == 0)
    def _():
        south[...] = jnp.zeros_like(south)

    @pl.when(cell == n_cell - 1)
    def _():
        north[...] = jnp.zeros_like(north)

    row_total = rows * n_cell

    def one_table_row(i, carry):
        row = cell * rows + i - HALO
        inside = jnp.where((row >= 0) & (row < row_total), 1.0, 0.0)
        band = jnp.minimum(jnp.maximum(row, 0), row_total - 1) // BAND
        for s in range(SUBSTEPS):
            regime = regime_ref[s, band]
            cx, cy = wind_ref[0, regime], wind_ref[1, regime]
            x_up, x_down = jnp.maximum(cx, 0.0), jnp.minimum(cx, 0.0)
            y_up, y_down = jnp.maximum(cy, 0.0), jnp.minimum(cy, 0.0)
            table[s * 5, i] = inside * (1.0 - 4.0 * DIFFUSION - x_up + x_down - y_up + y_down)
            table[s * 5 + 1, i] = inside * (x_up + DIFFUSION)
            table[s * 5 + 2, i] = inside * (DIFFUSION - x_down)
            table[s * 5 + 3, i] = inside * (y_up + DIFFUSION)
            table[s * 5 + 4, i] = inside * (DIFFUSION - y_down)
        return carry

    lax.fori_loop(0, rows + 2 * HALO, one_table_row, 0)

    lane = lax.broadcasted_iota(jnp.int32, (CHUNK, width), 1)

    def stencil(f):
        @pl.when(has_south)
        def _():
            upward(f).wait_recv()

        @pl.when(has_north)
        def _():
            downward(f).wait_recv()

        def one_chunk(step_at, carry):
            at = pl.ds(pl.multiple_of(step_at * CHUNK, CHUNK), CHUNK)
            cells = [south[f, i, at, :].astype(jnp.float32) for i in range(HALO)]
            cells += [x_ref[f, i, at, :] for i in range(rows)]
            cells += [north[f, i, at, :].astype(jnp.float32) for i in range(HALO)]
            for s in range(SUBSTEPS):
                fresh = list(cells)
                for i in range(s + 1, rows + 2 * HALO - s - 1):
                    q = cells[i]
                    west = jnp.where(lane == 0, 0.0, pltpu.roll(q, 1, 1))
                    east = jnp.where(lane == width - 1, 0.0, pltpu.roll(q, width - 1, 1))
                    fresh[i] = (
                        q * table[s * 5, i]
                        + cells[i - 1] * table[s * 5 + 1, i]
                        + cells[i + 1] * table[s * 5 + 2, i]
                        + west * table[s * 5 + 3, i]
                        + east * table[s * 5 + 4, i]
                    )
                cells = fresh
            for i in range(rows):
                pieces[member, f, i, at, :] = cells[HALO + i].astype(jnp.bfloat16)
                if f == 0:
                    keep[i, at, :] = cells[HALO + i]
            return carry

        lax.fori_loop(0, count // CHUNK, one_chunk, 0)

    column = lax.broadcasted_iota(jnp.int32, (width, slots), 0)

    def mark_row(i, carry):
        hit = jnp.where(column == index_ref[...] - i * width, 1.0, 0.0)
        hits[i] = hit.astype(jnp.bfloat16)
        return carry

    lax.fori_loop(0, rows, mark_row, 0)
    stencil(0)
    pred[...] = jnp.zeros_like(pred)

    def pick_row(i, carry):
        picked = jnp.dot(
            jnp.concatenate(split3(keep[i]), axis=0),
            hits[i],
            preferred_element_type=jnp.float32,
        )
        pred[...] += picked[:count] + picked[count : 2 * count] + picked[2 * count :]
        return carry

    lax.fori_loop(0, rows, pick_row, 0)

    def share_pred(d):
        peer = lax.rem(member + d, n_member)
        return remote(pred, everyone.at[own], send_pred.at[d], recv_pred.at[d], member=peer)

    def share_part(d):
        peer = lax.rem(cell + d, n_cell)
        return remote(mine, others.at[d - 1], send_part.at[d], recv_part.at[d], cell=peer)

    def share_gram(d):
        peer = lax.rem(member + d, n_member)
        src = total.at[pl.ds(0, count)]
        return remote(src, gram.at[own], send_gram.at[d], recv_gram.at[d], member=peer)

    for d in range(1, n_member):
        share_pred(d).start()
    everyone[own, :] = pred[...]
    send_field(0)
    if fields > 1:
        stencil(1)
    for d in range(1, n_member):
        share_pred(d).wait()

    predicted = everyone[...]
    ybar = jnp.mean(predicted, axis=0, keepdims=True)
    live = lax.broadcasted_iota(jnp.int32, (1, slots), 1) < count_ref[0]
    weight = jnp.where(live, 1.0, 0.0) / jnp.sqrt(var_ref[...])
    scaled = (predicted - ybar) * weight
    local = (pred[...] - ybar) * weight
    innovation = jnp.broadcast_to(weight * (value_ref[...] - ybar), (8, slots))
    mine[...] = nt_dot(jnp.concatenate([local, innovation], axis=0), scaled)
    for d in range(1, n_cell):
        share_part(d).start()
    for f in range(2, fields):
        stencil(f)
    for d in range(1, n_cell):
        share_part(d).wait()
    summed = mine[...]
    for d in range(n_cell - 1):
        summed = summed + others[d]
    total[...] = summed
    for d in range(1, n_member):
        share_gram(d).start()
    for f in range(1, fields):
        send_field(f)
    gram[own, :] = total[pl.ds(0, count), :]
    for d in range(1, n_member):
        share_gram(d).wait()

    lines = lax.broadcasted_iota(jnp.int32, (members, members), 0)
    columns = lax.broadcasted_iota(jnp.int32, (members, members), 1)
    identity = jnp.where(lines == columns, 1.0, 0.0).astype(jnp.float32)
    precision = gram[...] + (members - 1.0) * identity
    scale = jnp.sum(jnp.sum(precision * identity, axis=1, keepdims=True), axis=0, keepdims=True)
    upper[...] = precision / scale
    lower[...] = identity

    def newton(step, carry):
        y, z = split3(upper[...]), split3(lower[...])
        middle = split3(1.5 * identity - 0.5 * six_products(z, y))
        upper[...] = six_products(y, middle)
        lower[...] = six_products(middle, z)
        return carry

    for f in range(fields):
        lax.fori_loop(ROOT_STEPS * f // fields, ROOT_STEPS * (f + 1) // fields, newton, 0)
        forward_field(f)

    gain = total[pl.ds(count, 8), :]
    half_way = nt_dot(gain, lower[...])
    mean_weights = nt_dot(half_way, lower[...])[0:1, :] / scale
    root = jnp.sqrt((members - 1.0) / scale) * lower[own, :]
    blend = mean_weights + root
    transform = blend - jnp.mean(blend, axis=1, keepdims=True) + 1.0 / members
    coeff[...] = transform.astype(jnp.bfloat16)

    for f in range(fields):
        for d in range(chips):
            to_mate(d, f).wait()
        for d in range(1, chips):
            to_far(d, f).wait_send()

        def blend_row(r, carry):
            block = pieces[:, f, r].reshape(members, width)
            out_ref[f, r] = jnp.dot(coeff[...], block, preferred_element_type=jnp.float32)
            return carry

        lax.fori_loop(0, rows, blend_row, 0)

    for f in range(fields):

        @pl.when(has_north)
        def _():
            upward(f).wait_send()

        @pl.when(has_south)
        def _():
            downward(f).wait_send()


def shards(prior_sample_set, wind_table, regimes, obs_index, obs_count, obs_value, obs_var):
    n_cell, n_member = lax.axis_size("cell"), lax.axis_size("member")
    count, fields, rows, width = prior_sample_set.shape
    slots = obs_index.shape[1]
    members = count * n_member
    cells = prior_sample_set.transpose(1, 2, 0, 3)
    smem = pl.BlockSpec(memory_space=pltpu.SMEM)
    vmem = pl.BlockSpec(memory_space=pltpu.VMEM)
    single, half = jnp.float32, jnp.bfloat16
    edge = pltpu.VMEM((fields, HALO, count, width), half)
    square = pltpu.VMEM((members, members), single)
    part = (count + 8, members)
    dma = pltpu.SemaphoreType.DMA
    blended = pl.pallas_call(
        functools.partial(cycle_kernel, n_cell, n_member),
        in_specs=[smem] * 3 + [vmem] * 4,
        out_specs=vmem,
        out_shape=jax.ShapeDtypeStruct(cells.shape, single),
        scratch_shapes=[
            pltpu.SMEM((SUBSTEPS * 5, rows + 2 * HALO), single),
            pltpu.VMEM((rows, width, slots), half),
            pltpu.VMEM((rows, count, width), single),
            edge,
            edge,
            edge,
            edge,
            pltpu.VMEM((n_member, fields, rows, count, width), half),
            pltpu.VMEM((count, slots), single),
            pltpu.VMEM((count, members), half),
            pltpu.VMEM((members, slots), single),
            pltpu.VMEM(part, single),
            pltpu.VMEM((n_cell - 1,) + part, single),
            pltpu.VMEM(part, single),
            square,
            square,
            square,
        ]
        + [dma((fields,))] * 4
        + [dma((n_member,))] * 2
        + [dma((n_cell,))] * 2
        + [dma((n_member,))] * 2
        + [dma((n_member // 2, fields))] * 4,
        compiler_params=pltpu.CompilerParams(
            collective_id=0, has_side_effects=True, vmem_limit_bytes=VMEM_LIMIT
        ),
    )(regimes.T, wind_table.T, obs_count, obs_index, obs_value, obs_var, cells)
    return blended.transpose(2, 0, 1, 3)


def solution(mesh):
    return jax.shard_map(
        shards,
        mesh=mesh,
        in_specs=(
            P(("groups", "member"), None, "cell", None),
            P(),
            P("groups", None),
            P(("groups", "cell"), None),
            P(("groups", "cell")),
            P(("groups", "cell"), None),
            P(("groups", "cell"), None),
        ),
        out_specs=P(("groups", "member"), None, "cell", None),
        check_vma=False,
    )
```
